32 devices in a mesh: group: 2 (over x), tp: 16 (over z, y, core), pool: 1.
Axes of the slice: x: 2, y: 2, z: 4, core: 2. Of those that a mesh axis runs over, the one named last changes fastest.
Arguments:
- prompt_x: bfloat16 [2048, 8192], P(('group', 'pool'), 'tp'), parts along dimension 0, may hold values from -6 to 6
- decode_x: bfloat16 [4, 32, 8192], P(None, ('group', 'pool'), 'tp'), parts along dimension 1, may hold values from -240 to 240
- w_query: bfloat16 [8192, 8192], P(None, 'tp'), may hold values from -0.0625 to 0.0625
- w_keyval: bfloat16 [8192, 2048], P('tp'), may hold values from -0.0625 to 0.0625
- w_out: bfloat16 [8192, 8192], P('tp'), may hold values from -0.0625 to 0.0625
- prompt_blocks: int32 [32], P('group'), parts along dimension 0, may hold values from 1 to 32, 64 in all
- prompt_row: int32 [32], P('group'), parts along dimension 0, may hold values from 0 to 15, each once
Outputs:
- decode_out: bfloat16 [4, 32, 8192], P(None, ('group', 'pool'), 'tp'), parts along dimension 1
The draws below stay inside these ranges and needn't reach their ends.
There are 2 independent parts, one for each index of `group`. The reference program is written for one: setup_inputs(seed, part) draws one part's arguments, and reference() takes and returns one part's arrays. A program takes and returns all parts, laid end to end along the dimension named above; an argument that names none is the same for every part. Nothing has to cross between parts.
Inputs may be any that keep to these rules, and one draw needn't show every extreme that they name: `prompt_blocks`: each prompt has at least one block, the prompts fill the span exactly, and one prompt has exactly 32 blocks. `prompt_row`: every decode row continues exactly one prompt.
All inputs are finite; a program needn't handle non-finite values. Where the reference program divides by a largest or mean magnitude, that divisor is 1e-20 or more.
Results may differ from the reference program's by a relative error of at most 0.018.
Values may be sent and summed in bfloat16 or wider, within the bound.
No kernel may reach another device: no remote copies, remote signals or barrier semaphores. Data moves between devices by JAX's collectives and lax.ppermute only.
A program may use at most 128 MiB of HBM per device.

```python
import math
import jax
import jax.numpy as jnp
import numpy as np
from jax import lax

D = 8192
HQ = 64
KVH = 8
HD = 128
BLK = 16
STEPS = 4
MOSTB = 32
PRE_TOK = 1024
NBLK = 64
ROWS = 16


def draw_decode_x(key, part):
    base = jnp.clip(jax.random.normal(key, (STEPS, ROWS, D), jnp.float32), -6.0, 6.0)
    return base.astype(jnp.bfloat16)


def steps_of(rng, dims, split, smallest, largest):
    def one(dim, blocks):
        heights = jax.random.uniform(jax.random.fold_in(jax.random.fold_in(rng, 6), dim), (blocks,), jnp.float32, smallest / len(split), largest / len(split))
        return jnp.repeat(jnp.exp(heights), dims[dim] // blocks).reshape((-1,) + (1,) * (len(dims) - dim - 1))

    factor_of = one(*split[0])
    for cut in split[1:]:
        factor_of = factor_of * one(*cut)
    return factor_of


def length_profile(amount, total, reach, slope):
    weights = [(1 << 20) // math.isqrt(grade ** slope) + 1 for grade in range(2, amount + 1)]
    surplus, counts = total - reach - (amount - 1), [1] * (amount - 1)
    while surplus > 0:
        free = [i for i in range(amount - 1) if counts[i] < reach]
        pool, left = sum([weights[i] for i in free]), surplus
        for i in free:
            addition = min(reach - counts[i], max(1, left * weights[i] // pool), surplus)
            counts[i] = counts[i] + addition
            surplus = surplus - addition
    return np.array([reach] + counts)


def ragged_sizes(stream_key, count, total, most, lean):
    if count == 2:
        one = jax.random.randint(stream_key, (), max(1, total - most), min(most, total - 1) + 1)
        return jnp.stack([one, total - one])
    lengths = jnp.asarray(length_profile(count, total, most, lean), jnp.int32)
    twos = (count - 1) // 2
    source_of, taker = lengths[1:1 + 2 * twos:2], lengths[2:2 + 2 * twos:2]
    slack = jnp.minimum(source_of - 1, most - taker)
    shifted = jax.random.randint(jax.random.fold_in(stream_key, 1), (twos,), 0, 1 << 20) % (slack + 1)
    lengths = lengths.at[1:1 + 2 * twos:2].set(source_of - shifted).at[2:2 + 2 * twos:2].set(taker + shifted)
    return lengths[jax.random.permutation(jax.random.fold_in(stream_key, 2), count)]


def normal_values(rng, shape, spread, reach, pieces=(), held_as=jnp.bfloat16):
    array = spread * jax.random.normal(rng, shape, jnp.float32)
    if pieces:
        array = array * steps_of(rng, shape, pieces, -0.22, 0.18)
    return jnp.clip(array, -reach, reach).astype(held_as)


def setup_inputs(seed: int = 0, part: int = 0) -> dict:
    seeds = jax.random.split(jax.random.key(seed), 8)
    own_keys = jax.random.split(jax.random.fold_in(seeds[7], part), 8)
    prompt_x = normal_values(own_keys[0], (PRE_TOK, D), 1.0, 6.0, ((1, 16),))
    decode_x = draw_decode_x(jax.random.fold_in(jax.random.fold_in(seeds[7], part), 71), part)
    w_query = normal_values(seeds[2], (D, HQ * HD), D ** -0.5, 0.0625, ((1, 16),))
    w_keyval = normal_values(seeds[3], (D, KVH * 2 * HD), D ** -0.5, 0.0625, ((0, 16),))
    w_out = normal_values(seeds[4], (HQ * HD, D), (HQ * HD) ** -0.5, 0.0625, ((0, 16),))
    prompt_blocks = ragged_sizes(own_keys[5], ROWS, NBLK, MOSTB, 2).astype(jnp.int32)
    prompt_row = jax.random.permutation(own_keys[6], ROWS).astype(jnp.int32)
    return dict(prompt_x=prompt_x, decode_x=decode_x, w_query=w_query, w_keyval=w_keyval, w_out=w_out, prompt_blocks=prompt_blocks, prompt_row=prompt_row)


def block_rows(prompt_blocks, prompt_row, total_blocks):
    block_ends = jnp.cumsum(prompt_blocks).astype(jnp.int32)
    positions = jnp.arange(total_blocks, dtype=jnp.int32)
    owner_seq = lax.optimization_barrier(jnp.sum((block_ends[None, :] <= positions[:, None]).astype(jnp.int32), axis=1))
    seq_match = owner_seq[:, None] == jnp.arange(prompt_row.shape[0], dtype=jnp.int32)[None, :]
    return lax.optimization_barrier(jnp.sum(jnp.where(seq_match, prompt_row[None, :], 0), axis=1)).astype(jnp.int32)

def attend(queries, cache_vals, cache_scale, slot_row, fresh_keyval, row_ids):
    head_dim = queries.shape[-1]
    inverse_root = 1.0 / math.sqrt(head_dim)
    query_f32 = queries.astype(jnp.float32)
    scale_f32 = cache_scale.astype(jnp.float32)
    cache_keys = cache_vals[:, :, :head_dim].astype(jnp.float32) * scale_f32[:, 0][:, None, None]
    cache_values = cache_vals[:, :, head_dim:].astype(jnp.float32) * scale_f32[:, 1][:, None, None]
    cache_score = jnp.einsum('srgd,nkd->srgnk', query_f32, cache_keys) * inverse_root
    visible = slot_row[None, :] == row_ids[:, None]
    cache_score = jnp.where(visible[None, :, None, :, None], cache_score, -jnp.inf)
    fresh_f32 = fresh_keyval.astype(jnp.float32)
    fresh_score = jnp.einsum('srgd,trd->srgt', query_f32, fresh_f32[:, :, :head_dim]) * inverse_root
    step_index = jnp.arange(queries.shape[0], dtype=jnp.int32)
    causal = step_index[:, None] >= step_index[None, :]
    fresh_score = jnp.where(causal[:, None, None, :], fresh_score, -jnp.inf)
    top_score = jnp.maximum(lax.optimization_barrier(jnp.max(cache_score, axis=(3, 4))), lax.optimization_barrier(jnp.max(fresh_score, axis=3)))
    cache_weight = jnp.exp(cache_score - top_score[..., None, None])
    fresh_weight = jnp.exp(fresh_score - top_score[..., None])
    denominator = lax.optimization_barrier(jnp.sum(cache_weight, axis=(3, 4))) + lax.optimization_barrier(jnp.sum(fresh_weight, axis=3))
    weighted = jnp.einsum('srgnk,nkd->srgd', cache_weight, cache_values)
    weighted = weighted + jnp.einsum('srgt,trd->srgd', fresh_weight, fresh_f32[:, :, head_dim:])
    return weighted / denominator[..., None]

def reference(prompt_x, decode_x, w_query, w_keyval, w_out, prompt_blocks, prompt_row):
    keyval = jnp.dot(prompt_x, w_keyval, preferred_element_type=jnp.float32)
    total_blocks = keyval.shape[0] // BLK
    blocked = keyval.reshape(total_blocks, BLK, KVH, 2, HD)
    scales = (lax.optimization_barrier(jnp.max(jnp.abs(blocked), axis=(1, 4))) + 1e-06).astype(jnp.bfloat16)
    stored = (blocked / scales.astype(jnp.float32)[:, None, :, :, None]).astype(jnp.bfloat16)
    stored = stored.reshape(total_blocks, BLK, KVH, 2 * HD).transpose(2, 0, 1, 3)
    scales = scales.transpose(1, 0, 2)
    slot_row = block_rows(prompt_blocks, prompt_row, total_blocks)
    step_count, row_count, model_width = decode_x.shape
    flat_rows = decode_x.reshape(step_count * row_count, model_width)
    queries = jnp.dot(flat_rows, w_query, preferred_element_type=jnp.float32).astype(jnp.bfloat16)
    queries = queries.reshape(step_count, row_count, KVH, HQ // KVH, HD).transpose(2, 0, 1, 3, 4)
    fresh_keyval = jnp.dot(flat_rows, w_keyval, preferred_element_type=jnp.float32).astype(jnp.bfloat16)
    fresh_keyval = fresh_keyval.reshape(step_count, row_count, KVH, 2 * HD).transpose(2, 0, 1, 3)
    row_ids = jnp.arange(row_count, dtype=jnp.int32)

    def per_head(head_inputs):
        return attend(head_inputs[0], head_inputs[1], head_inputs[2], slot_row, head_inputs[3], row_ids)
    weighted = lax.map(per_head, (queries, stored, scales, fresh_keyval))
    attended = weighted.transpose(1, 2, 0, 3, 4).reshape(step_count * row_count, HQ * HD).astype(jnp.bfloat16)
    decode_out = jnp.dot(attended, w_out, preferred_element_type=jnp.float32).astype(jnp.bfloat16)
    return decode_out.reshape(step_count, row_count, model_width)
```

```python
import functools
import math

import jax
import jax.numpy as jnp
import numpy as np
from jax import lax
from jax.experimental import pallas as pl
from jax.experimental.pallas import tpu as pltpu
from jax.sharding import PartitionSpec as P

KVH = 8
HD = 128
BLK = 16
F32 = jnp.float32
BF16 = jnp.bfloat16


def block_rows(prompt_blocks, prompt_row, total_blocks):
    block_ends = jnp.cumsum(prompt_blocks)
    positions = jnp.arange(total_blocks, dtype=jnp.int32)
    owner_seq = jnp.sum((block_ends[None, :] <= positions[:, None]).astype(jnp.int32), axis=1)
    seq_match = owner_seq[:, None] == jnp.arange(prompt_row.shape[0], dtype=jnp.int32)[None, :]
    return jnp.sum(jnp.where(seq_match, prompt_row[None, :], 0), axis=1)


def attend(queries, cache_vals, cache_scale, slot_row, fresh_keyval, row_ids):
    head_dim = queries.shape[-1]
    inverse_root = 1.0 / math.sqrt(head_dim)
    query_f32 = queries.astype(jnp.float32)
    scale_f32 = cache_scale.astype(jnp.float32)
    cache_keys = cache_vals[:, :, :head_dim].astype(jnp.float32) * scale_f32[:, 0][:, None, None]
    cache_values = cache_vals[:, :, head_dim:].astype(jnp.float32) * scale_f32[:, 1][:, None, None]
    cache_score = jnp.einsum("srgd,nkd->srgnk", query_f32, cache_keys) * inverse_root
    visible = slot_row[None, :] == row_ids[:, None]
    cache_score = jnp.where(visible[None, :, None, :, None], cache_score, -jnp.inf)
    fresh_f32 = fresh_keyval.astype(jnp.float32)
    fresh_score = jnp.einsum("srgd,trd->srgt", query_f32, fresh_f32[:, :, :head_dim]) * inverse_root
    step_index = jnp.arange(queries.shape[0], dtype=jnp.int32)
    causal = step_index[:, None] >= step_index[None, :]
    fresh_score = jnp.where(causal[:, None, None, :], fresh_score, -jnp.inf)
    top_score = jnp.maximum(jnp.max(cache_score, axis=(3, 4)), jnp.max(fresh_score, axis=3))
    cache_weight = jnp.exp(cache_score - top_score[..., None, None])
    fresh_weight = jnp.exp(fresh_score - top_score[..., None])
    denominator = jnp.sum(cache_weight, axis=(3, 4)) + jnp.sum(fresh_weight, axis=3)
    weighted = jnp.einsum("srgnk,nkd->srgd", cache_weight, cache_values)
    weighted = weighted + jnp.einsum("srgt,trd->srgd", fresh_weight, fresh_f32[:, :, head_dim:])
    return weighted / denominator[..., None]


def general(prompt_x, decode_x, w_query, w_keyval, w_out, prompt_blocks, prompt_row):
    tp_count = lax.axis_size("tp")
    pool_count = lax.axis_size("pool")
    tp_index = lax.axis_index("tp")
    pool_index = lax.axis_index("pool")
    half_tokens = prompt_x.shape[0]
    tokens_here = half_tokens // tp_count
    blocks_here = tokens_here // BLK
    half_blocks = half_tokens // BLK
    total_blocks = half_blocks * pool_count
    keyval = lax.psum_scatter(
        jnp.dot(prompt_x, w_keyval, preferred_element_type=jnp.float32),
        "tp",
        scatter_dimension=0,
        tiled=True,
    )
    blocked = keyval.reshape(blocks_here, BLK, KVH, 2, HD)
    scales = (jnp.max(jnp.abs(blocked), axis=(1, 4)) + 1e-06).astype(jnp.bfloat16)
    stored = (blocked / scales.astype(jnp.float32)[:, None, :, :, None]).astype(jnp.bfloat16)
    stored = stored.reshape(blocks_here, BLK, KVH, 2 * HD)
    slot_row_all = block_rows(prompt_blocks, prompt_row, total_blocks)
    row_half = decode_x.shape[1]
    owner_half = slot_row_all // row_half
    first_block = pool_index * half_blocks + tp_index * blocks_here
    mine_owner = lax.dynamic_slice_in_dim(owner_half, first_block, blocks_here, 0)
    dest_head = np.arange(tp_count) * KVH // tp_count
    by_head = stored.transpose(2, 0, 1, 3)[dest_head]
    scale_head = scales.transpose(1, 0, 2)[dest_head]
    to_half = mine_owner[None, :] == jnp.arange(pool_count, dtype=jnp.int32)[:, None]
    zero_value = jnp.zeros((), jnp.bfloat16)
    send_vals = jnp.where(to_half[None, :, :, None, None], by_head[:, None], zero_value)
    send_scale = jnp.where(to_half[None, :, :, None], scale_head[:, None], zero_value)
    got_vals, got_scale = (
        lax.all_to_all(
            lax.all_to_all(sent, "tp", split_axis=0, concat_axis=0, tiled=True),
            "pool",
            split_axis=1,
            concat_axis=1,
            tiled=True,
        )
        for sent in (send_vals, send_scale)
    )
    got_vals = got_vals.reshape(total_blocks, BLK, 2 * HD)
    got_scale = got_scale.reshape(total_blocks, 2)
    slot_row = (
        slot_row_all.reshape(pool_count, tp_count, blocks_here)
        .transpose(1, 0, 2)
        .reshape(total_blocks)
    )
    gathered = lax.all_gather(decode_x, "tp", axis=2, tiled=True)
    step_count, row_count, model_width = gathered.shape
    heads_here = w_query.shape[1] // HD
    queries = jnp.einsum("srd,de->sre", gathered, w_query, preferred_element_type=jnp.float32)
    queries = queries.astype(jnp.bfloat16).reshape(step_count, row_count, heads_here, HD)
    partial_new = jnp.einsum("srd,de->sre", decode_x, w_keyval, preferred_element_type=jnp.float32)
    summed_new = lax.psum(partial_new, "tp")
    fresh_keyval = summed_new.astype(jnp.bfloat16).reshape(step_count, row_count, KVH, 2 * HD)
    my_head = tp_index * KVH // tp_count
    fresh_keyval = lax.dynamic_index_in_dim(fresh_keyval, my_head, 2, keepdims=False)
    row_ids = pool_index * row_count + jnp.arange(row_count, dtype=jnp.int32)
    weighted = attend(queries, got_vals, got_scale, slot_row, fresh_keyval, row_ids)
    attended = weighted.reshape(step_count, row_count, heads_here * HD).astype(jnp.bfloat16)
    out_term = jnp.einsum("sre,ed->srd", attended, w_out, preferred_element_type=jnp.float32)
    return lax.psum_scatter(out_term, "tp", scatter_dimension=2, tiled=True).astype(jnp.bfloat16)


VM = pl.BlockSpec(memory_space=pltpu.VMEM)
SM = pl.BlockSpec(memory_space=pltpu.SMEM)
HB = pl.BlockSpec(memory_space=pl.ANY)
VLIM = 48 << 20


def cost(flops, nbytes):
    return pl.CostEstimate(flops=int(flops), bytes_accessed=int(nbytes), transcendentals=0)


def struct(shape, dtype):
    return jax.ShapeDtypeStruct(shape, dtype)


def swap(x, mask, count):
    return lax.ppermute(x, "tp", [(i, i ^ mask) for i in range(count)])


def dot(a, b):
    return jnp.dot(a, b, preferred_element_type=F32)


def pick_columns(w, blocks, width, name):
    rows = w.shape[0]
    count = blocks.shape[0]

    def kernel(idx_ref, w_ref, o_ref, sem):
        copies = [
            pltpu.make_async_copy(
                w_ref.at[:, pl.ds(pl.multiple_of(idx_ref[i] * width, width), width)],
                o_ref.at[:, pl.ds(i * width, width)],
                sem.at[i],
            )
            for i in range(count)
        ]
        for c in copies:
            c.start()
        for c in copies:
            c.wait()

    return pl.pallas_call(
        kernel,
        out_shape=struct((rows, count * width), w.dtype),
        in_specs=[SM, HB],
        out_specs=VM,
        scratch_shapes=[pltpu.SemaphoreType.DMA((count,))],
        compiler_params=pltpu.CompilerParams(vmem_limit_bytes=VLIM),
        cost_estimate=cost(0, 4 * rows * count * width),
        name=name,
    )(blocks, w)


def kv_remote(x0, x1, d0, d1, w0, w1, rows_a):
    tokens, fresh = x0.shape[0], d0.shape[0]
    rows_b = tokens - rows_a + fresh
    half = 4 * HD

    def kernel(x0, x1, d0, d1, w0, w1, a_ref, b1, b2, b3):
        a_ref[...] = (
            dot(x0[:rows_a, :], w0[:, half:]) + dot(x1[:rows_a, :], w1[:, half:])
        ).astype(BF16)
        for k, b in ((1, b1), (2, b2), (3, b3)):
            for j in range(2):
                cols = slice(j * half + k * HD, j * half + (k + 1) * HD)
                b[: tokens - rows_a, j * HD : (j + 1) * HD] = (
                    dot(x0[rows_a:, :], w0[:, cols]) + dot(x1[rows_a:, :], w1[:, cols])
                ).astype(BF16)
                b[tokens - rows_a :, j * HD : (j + 1) * HD] = (
                    dot(d0[...], w0[:, cols]) + dot(d1[...], w1[:, cols])
                ).astype(BF16)

    return pl.pallas_call(
        kernel,
        out_shape=[struct((rows_a, half), BF16)] + [struct((rows_b, 2 * HD), BF16)] * 3,
        in_specs=[VM] * 6,
        out_specs=[VM] * 4,
        compiler_params=pltpu.CompilerParams(vmem_limit_bytes=VLIM),
        cost_estimate=cost(2e9, 6e6),
        name="kv_remote",
    )(x0, x1, d0, d1, w0, w1)


def kv_local(x0, x1, d0, d1, w0, w1, rows_a):
    tokens, fresh = x0.shape[0], d0.shape[0]
    rows_b = tokens - rows_a + fresh
    half = 4 * HD

    def kernel(x0, x1, d0, d1, w0, w1, a_ref, b_ref):
        a_ref[...] = dot(x0[:rows_a, :], w0[:, :half]) + dot(x1[:rows_a, :], w1[:, :half])
        for j in range(2):
            cols = slice(j * half, j * half + HD)
            b_ref[: tokens - rows_a, j * HD : (j + 1) * HD] = dot(
                x0[rows_a:, :], w0[:, cols]
            ) + dot(x1[rows_a:, :], w1[:, cols])
            b_ref[tokens - rows_a :, j * HD : (j + 1) * HD] = dot(d0[...], w0[:, cols]) + dot(
                d1[...], w1[:, cols]
            )

    return pl.pallas_call(
        kernel,
        out_shape=[struct((rows_a, half), F32), struct((rows_b, 2 * HD), F32)],
        in_specs=[VM] * 6,
        out_specs=[VM] * 2,
        compiler_params=pltpu.CompilerParams(vmem_limit_bytes=VLIM),
        cost_estimate=cost(1.5e9, 6e6),
        name="kv_local",
    )(x0, x1, d0, d1, w0, w1)


def mid_a(own, got):
    rows = own.shape[0]

    def kernel(own, got, m_ref, z1, z2, z3):
        for k, ref in ((0, m_ref), (1, z1), (2, z2), (3, z3)):
            cols = slice(k * HD, (k + 1) * HD)
            ref[...] = (own[:, cols] + got[:, cols].astype(F32)).astype(ref.dtype)

    return pl.pallas_call(
        kernel,
        out_shape=[struct((rows, HD), F32)] + [struct((rows, HD), BF16)] * 3,
        in_specs=[VM] * 2,
        out_specs=[VM] * 4,
        cost_estimate=cost(1e6, 4e6),
        name="mid_a",
    )(own, got)


def mid_b(own, g1, g2, g3):
    rows = own.shape[0]

    def kernel(own, g1, g2, g3, m_ref, y_ref):
        for j, ref in ((0, m_ref), (1, y_ref)):
            cols = slice(j * HD, (j + 1) * HD)
            total = own[:, cols]
            for g in (g1, g2, g3):
                total = total + g[:, cols].astype(F32)
            ref[...] = total.astype(ref.dtype)

    return pl.pallas_call(
        kernel,
        out_shape=[struct((rows, HD), F32), struct((rows, HD), BF16)],
        in_specs=[VM] * 4,
        out_specs=[VM] * 2,
        cost_estimate=cost(1e6, 3e6),
        name="mid_b",
    )(own, g1, g2, g3)


def finish_kv(a_own, a1, a2, a3, b_own, b1, tokens):
    rows_a, rows_b = a_own.shape[0], b_own.shape[0]
    blocks = tokens // BLK
    rows = rows_a + rows_b

    def kernel(a_own, a1, a2, a3, b_own, b1, o_ref):
        a = a_own[...] + a1[...].astype(F32) + a2[...].astype(F32) + a3[...].astype(F32)
        b = b_own[...] + b1[...].astype(F32)
        for v, first in ((a, 0), (b[: tokens - rows_a], rows_a)):
            n = v.shape[0] // BLK
            v = v.reshape(n, BLK, HD)
            top = jnp.max(jnp.max(jnp.abs(v), axis=1, keepdims=True), axis=2, keepdims=True)
            scale = (top + 1e-06).astype(BF16)
            wide = jnp.broadcast_to(scale.astype(F32), (n, 1, HD))
            o_ref[first : first + n * BLK, :] = (v / wide).astype(BF16).reshape(n * BLK, HD)
            o_ref[rows + first // BLK : rows + first // BLK + n, :] = wide.reshape(n, HD).astype(
                BF16
            )
        o_ref[tokens:rows, :] = b[tokens - rows_a :].astype(BF16)

    return pl.pallas_call(
        kernel,
        out_shape=struct((rows + blocks, HD), BF16),
        in_specs=[VM] * 6,
        out_specs=VM,
        cost_estimate=cost(1e6, 2e6),
        name="finish_kv",
    )(a_own, a1, a2, a3, b_own, b1)


def queries_of(s0, s0o, s1, s1o, w_query, chip, core):
    rows, width = s0.shape[1:]
    cols = w_query.shape[1]
    order = jnp.stack(
        [chip ^ (2 * (i % 4) + i // 4) for i in range(8)] + [core]
    ).astype(jnp.int32)

    def kernel(ord_ref, a0, a0o, a1, a1o, w_ref, o_ref, acc):
        i = pl.program_id(0)
        c = ord_ref[8]
        k = lax.rem(i, 4)
        near = i < 4
        w_own = w_ref[pl.ds(pl.multiple_of(c * width, width), width), :]
        w_oth = w_ref[pl.ds(pl.multiple_of((1 - c) * width, width), width), :]
        own = jnp.where(near, a0[k], a1[k])
        oth = jnp.where(near, a0o[k], a1o[k])
        term = dot(own, w_own) + dot(oth, w_oth)

        @pl.when(i == 0)
        def _():
            acc[...] = term

        @pl.when(i > 0)
        def _():
            acc[...] += term

        @pl.when(i == 7)
        def _():
            o_ref[...] = acc[...].astype(BF16)

    full = pl.BlockSpec((4, rows, width), lambda i, o: (0, 0, 0))
    return pl.pallas_call(
        kernel,
        grid_spec=pltpu.PrefetchScalarGridSpec(
            num_scalar_prefetch=1,
            grid=(8,),
            in_specs=[full] * 4 + [pl.BlockSpec((2 * width, cols), lambda i, o: (o[i], 0))],
            out_specs=pl.BlockSpec((rows, cols), lambda i, o: (0, 0)),
            scratch_shapes=[pltpu.VMEM((rows, cols), F32)],
        ),
        out_shape=struct((rows, cols), BF16),
        compiler_params=pltpu.CompilerParams(vmem_limit_bytes=VLIM),
        cost_estimate=cost(5e8, 9e6),
        name="queries",
    )(order, s0, s0o, s1, s1o, w_query)


def attend_out(q0, q1, kv0, kv1, marks, w_out, w_got, chip, core, tokens, row_count):
    rows, qcols = q0.shape
    heads = qcols // HD
    blocks = tokens // BLK
    slots = tokens + rows
    width = w_got.shape[1] // 8
    inverse_root = 1.0 / math.sqrt(HD)
    order = jnp.stack([2 * (chip ^ r) + core for r in range(7, -1, -1)] + [core]).astype(jnp.int32)

    def kernel(ord_ref, q0, q1, kv0, kv1, mk, w0, w1, o7, o6, o5, o4, o3, o2, o1, o0, att0, att1):
        i = pl.program_id(0)

        @pl.when(i == 0)
        def _():
            first = ord_ref[8] == 0

            def wide(kv):
                scale = kv[slots:, :].astype(F32).reshape(blocks, 1, HD)
                v = kv[:tokens, :].astype(F32).reshape(blocks, BLK, HD) * scale
                return v.reshape(tokens, HD).astype(BF16)

            own, oth = wide(kv0), wide(kv1)
            own_new, oth_new = kv0[tokens:slots, :], kv1[tokens:slots, :]
            keys = jnp.concatenate(
                [jnp.where(first, own, oth), jnp.where(first, own_new, oth_new)]
            )
            values = jnp.concatenate(
                [jnp.where(first, oth, own), jnp.where(first, oth_new, own_new)]
            )
            who = lax.broadcasted_iota(jnp.int32, (rows, slots), 0)
            seen = (lax.rem(who, row_count) == mk[0:1, :]) & (who >= mk[1:2, :])
            for q, att in ((q0, att0), (q1, att1)):
                stack = jnp.concatenate([q[:, g * HD : (g + 1) * HD] for g in range(heads)])
                score = lax.dot_general(
                    stack, keys, (((1,), (1,)), ((), ())), preferred_element_type=F32
                )
                score = score.reshape(heads, rows, slots) * inverse_root
                score = jnp.where(seen[None], score, -jnp.inf)
                top = jnp.max(score, axis=2, keepdims=True)
                weight = jnp.exp(score - top)
                total = jnp.sum(weight, axis=2, keepdims=True)
                mixed = dot(weight.astype(BF16).reshape(heads * rows, slots), values)
                mixed = mixed.reshape(heads, rows, HD) / total
                for g in range(heads):
                    att[:, g * HD : (g + 1) * HD] = mixed[g].astype(BF16)

        term = dot(att0[...], w0[...]) + dot(att1[...], w1[...])
        for step, ref in enumerate((o7, o6, o5, o4, o3, o2, o1, o0)):

            @pl.when(i == step)
            def _(ref=ref):
                ref[...] = term.astype(ref.dtype)

    def whole(x):
        return pl.BlockSpec(x.shape, lambda i, o: (0,) * x.ndim)

    out_block = pl.BlockSpec((rows, width), lambda i, o: (0, 0))
    return pl.pallas_call(
        kernel,
        grid_spec=pltpu.PrefetchScalarGridSpec(
            num_scalar_prefetch=1,
            grid=(8,),
            in_specs=[whole(q0), whole(q1), whole(kv0), whole(kv1), whole(marks)]
            + [
                pl.BlockSpec((w_out.shape[0], width), lambda i, o: (0, o[i])),
                pl.BlockSpec((w_got.shape[0], width), lambda i, o: (0, i)),
            ],
            out_specs=[out_block] * 8,
            scratch_shapes=[pltpu.VMEM((rows, qcols), BF16)] * 2,
        ),
        out_shape=[struct((rows, width), BF16)] * 7 + [struct((rows, width), F32)],
        compiler_params=pltpu.CompilerParams(vmem_limit_bytes=VLIM),
        cost_estimate=cost(2e9, 9e6),
        name="attend_out",
    )(order, q0, q1, kv0, kv1, marks, w_out, w_got)


def add_up(own, parts):
    def kernel(*refs):
        total = refs[0][...]
        for r in refs[1:-1]:
            total = total + r[...].astype(F32)
        refs[-1][...] = total.astype(BF16)

    return pl.pallas_call(
        kernel,
        out_shape=struct(own.shape, BF16),
        in_specs=[VM] * (1 + len(parts)),
        out_specs=VM,
        cost_estimate=cost(1e6, 1e6),
        name="add_up",
    )(own, *parts)


def paired(prompt_x, decode_x, w_query, w_keyval, w_out, prompt_blocks, prompt_row):
    count = lax.axis_size("tp")
    index = lax.axis_index("tp")
    core, chip = index % 2, index // 2
    tokens = prompt_x.shape[0]
    steps, row_count, depth = decode_x.shape
    fresh = steps * row_count
    total_blocks = tokens // BLK
    rows_a = (tokens + fresh) * 5 // 8 // 64 * 64
    d_own = decode_x.reshape(fresh, depth)
    move = functools.partial(swap, count=count)
    near = [move(d_own, 4 * k) for k in (3, 2, 1)]
    x_oth = move(prompt_x, 1)
    d_oth = move(d_own, 1)
    rel = [(i % 4) * 2 + i // 4 for i in range(8)]
    keep_cols = jnp.stack([(chip ^ r) * 2 + core for r in rel]).astype(jnp.int32)
    send_cols = jnp.stack([(chip ^ r) * 2 + 1 - core for r in rel]).astype(jnp.int32)
    w_send = pick_columns(w_keyval, send_cols, HD, "kv_columns_out")
    w_oth = move(w_send, 1)
    w_keep = pick_columns(w_keyval, keep_cols, HD, "kv_columns_own")
    a_send, b1, b2, b3 = kv_remote(prompt_x, x_oth, d_own, d_oth, w_keep, w_oth, rows_a)
    a_got = move(a_send, 2)
    g3, g2, g1 = move(b3, 12), move(b2, 8), move(b1, 4)
    a_own, b_own = kv_local(prompt_x, x_oth, d_own, d_oth, w_keep, w_oth, rows_a)
    s0 = jnp.stack([d_own, near[2], near[1], near[0]])
    s1 = move(s0, 2)
    s0_oth = move(s0, 1)
    a_own, a1, a2, a3 = mid_a(a_own, a_got)
    h3, h2, h1 = move(a3, 12), move(a2, 8), move(a1, 4)
    b_own, b_send = mid_b(b_own, g1, g2, g3)
    b_got = move(b_send, 2)
    s1_oth = move(s1, 1)
    q_own = queries_of(s0, s0_oth, s1, s1_oth, w_query, chip, core)
    q_oth = move(q_own, 1)
    width = w_out.shape[1] // count
    out_cols = jnp.stack([2 * (chip ^ r) + 1 - core for r in range(7, -1, -1)]).astype(jnp.int32)
    w_got = move(pick_columns(w_out, out_cols, width, "out_columns"), 1)
    slot_row = jnp.repeat(block_rows(prompt_blocks, prompt_row, total_blocks), BLK)
    new = jnp.arange(fresh, dtype=jnp.int32)
    marks = jnp.stack(
        [
            jnp.concatenate([slot_row, new % row_count]),
            jnp.concatenate([jnp.zeros_like(slot_row), new // row_count * row_count]),
        ]
    )
    kv_own = finish_kv(a_own, h1, h2, h3, b_own, b_got, tokens)
    kv_oth = move(kv_own, 1)
    *sends, mine = attend_out(
        q_own, q_oth, kv_own, kv_oth, marks, w_out, w_got, chip, core, tokens, row_count
    )
    parts = [move(s, 2 * r) for r, s in zip(range(7, 0, -1), sends)]
    return add_up(mine, parts).reshape(steps, row_count, width)


def solution(mesh):
    placed = (
        P(("group", "pool"), "tp"),
        P(None, ("group", "pool"), "tp"),
        P(None, "tp"),
        P("tp", None),
        P("tp", None),
        P("group"),
        P("group"),
    )
    pairs = mesh.shape["pool"] == 1 and mesh.shape["tp"] == 2 * KVH
    return jax.shard_map(
        paired if pairs else general,
        mesh=mesh,
        in_specs=placed,
        out_specs=P(None, ("group", "pool"), "tp"),
        check_vma=False,
    )
```

```python
import math

import jax
import jax.numpy as jnp
import numpy as np
from jax import lax
from jax.experimental import pallas as pl
from jax.experimental.pallas import tpu as pltpu
from jax.sharding import PartitionSpec as P


KVH = 8
HD = 128
BLK = 16
F32 = jnp.float32
BF16 = jnp.bfloat16


def block_rows(prompt_blocks, prompt_row, total_blocks):
    block_ends = jnp.cumsum(prompt_blocks)
    positions = jnp.arange(total_blocks, dtype=jnp.int32)
    owner_seq = jnp.sum((block_ends[None, :] <= positions[:, None]).astype(jnp.int32), axis=1)
    seq_match = owner_seq[:, None] == jnp.arange(prompt_row.shape[0], dtype=jnp.int32)[None, :]
    return jnp.sum(jnp.where(seq_match, prompt_row[None, :], 0), axis=1)


def attend(queries, cache_vals, cache_scale, slot_row, fresh_keyval, row_ids):
    head_dim = queries.shape[-1]
    inverse_root = 1.0 / math.sqrt(head_dim)
    query_f32 = queries.astype(jnp.float32)
    scale_f32 = cache_scale.astype(jnp.float32)
    cache_keys = cache_vals[:, :, :head_dim].astype(jnp.float32) * scale_f32[:, 0][:, None, None]
    cache_values = cache_vals[:, :, head_dim:].astype(jnp.float32) * scale_f32[:, 1][:, None, None]
    cache_score = jnp.einsum("srgd,nkd->srgnk", query_f32, cache_keys) * inverse_root
    visible = slot_row[None, :] == row_ids[:, None]
    cache_score = jnp.where(visible[None, :, None, :, None], cache_score, -jnp.inf)
    fresh_f32 = fresh_keyval.astype(jnp.float32)
    fresh_score = jnp.einsum("srgd,trd->srgt", query_f32, fresh_f32[:, :, :head_dim]) * inverse_root
    step_index = jnp.arange(queries.shape[0], dtype=jnp.int32)
    causal = step_index[:, None] >= step_index[None, :]
    fresh_score = jnp.where(causal[:, None, None, :], fresh_score, -jnp.inf)
    top_score = jnp.maximum(jnp.max(cache_score, axis=(3, 4)), jnp.max(fresh_score, axis=3))
    cache_weight = jnp.exp(cache_score - top_score[..., None, None])
    fresh_weight = jnp.exp(fresh_score - top_score[..., None])
    denominator = jnp.sum(cache_weight, axis=(3, 4)) + jnp.sum(fresh_weight, axis=3)
    weighted = jnp.einsum("srgnk,nkd->srgd", cache_weight, cache_values)
    weighted = weighted + jnp.einsum("srgt,trd->srgd", fresh_weight, fresh_f32[:, :, head_dim:])
    return weighted / denominator[..., None]


def general(prompt_x, decode_x, w_query, w_keyval, w_out, prompt_blocks, prompt_row):
    tp_count = lax.axis_size("tp")
    pool_count = lax.axis_size("pool")
    tp_index = lax.axis_index("tp")
    pool_index = lax.axis_index("pool")
    half_tokens = prompt_x.shape[0]
    tokens_here = half_tokens // tp_count
    blocks_here = tokens_here // BLK
    half_blocks = half_tokens // BLK
    total_blocks = half_blocks * pool_count
    keyval = lax.psum_scatter(
        jnp.dot(prompt_x, w_keyval, preferred_element_type=jnp.float32),
        "tp",
        scatter_dimension=0,
        tiled=True,
    )
    blocked = keyval.reshape(blocks_here, BLK, KVH, 2, HD)
    scales = (jnp.max(jnp.abs(blocked), axis=(1, 4)) + 1e-06).astype(jnp.bfloat16)
    stored = (blocked / scales.astype(jnp.float32)[:, None, :, :, None]).astype(jnp.bfloat16)
    stored = stored.reshape(blocks_here, BLK, KVH, 2 * HD)
    slot_row_all = block_rows(prompt_blocks, prompt_row, total_blocks)
    row_half = decode_x.shape[1]
    owner_half = slot_row_all // row_half
    first_block = pool_index * half_blocks + tp_index * blocks_here
    mine_owner = lax.dynamic_slice_in_dim(owner_half, first_block, blocks_here, 0)
    dest_head = np.arange(tp_count) * KVH // tp_count
    by_head = stored.transpose(2, 0, 1, 3)[dest_head]
    scale_head = scales.transpose(1, 0, 2)[dest_head]
    to_half = mine_owner[None, :] == jnp.arange(pool_count, dtype=jnp.int32)[:, None]
    zero_value = jnp.zeros((), jnp.bfloat16)
    send_vals = jnp.where(to_half[None, :, :, None, None], by_head[:, None], zero_value)
    send_scale = jnp.where(to_half[None, :, :, None], scale_head[:, None], zero_value)
    got_vals, got_scale = (
        lax.all_to_all(
            lax.all_to_all(sent, "tp", split_axis=0, concat_axis=0, tiled=True),
            "pool",
            split_axis=1,
            concat_axis=1,
            tiled=True,
        )
        for sent in (send_vals, send_scale)
    )
    got_vals = got_vals.reshape(total_blocks, BLK, 2 * HD)
    got_scale = got_scale.reshape(total_blocks, 2)
    slot_row = (
        slot_row_all.reshape(pool_count, tp_count, blocks_here)
        .transpose(1, 0, 2)
        .reshape(total_blocks)
    )
    gathered = lax.all_gather(decode_x, "tp", axis=2, tiled=True)
    step_count, row_count, _ = gathered.shape
    heads_here = w_query.shape[1] // HD
    queries = jnp.einsum("srd,de->sre", gathered, w_query, preferred_element_type=jnp.float32)
    queries = queries.astype(jnp.bfloat16).reshape(step_count, row_count, heads_here, HD)
    partial_new = jnp.einsum("srd,de->sre", decode_x, w_keyval, preferred_element_type=jnp.float32)
    summed_new = lax.psum(partial_new, "tp")
    fresh_keyval = summed_new.astype(jnp.bfloat16).reshape(step_count, row_count, KVH, 2 * HD)
    my_head = tp_index * KVH // tp_count
    fresh_keyval = lax.dynamic_index_in_dim(fresh_keyval, my_head, 2, keepdims=False)
    row_ids = pool_index * row_count + jnp.arange(row_count, dtype=jnp.int32)
    weighted = attend(queries, got_vals, got_scale, slot_row, fresh_keyval, row_ids)
    attended = weighted.reshape(step_count, row_count, heads_here * HD).astype(jnp.bfloat16)
    out_term = jnp.einsum("sre,ed->srd", attended, w_out, preferred_element_type=jnp.float32)
    return lax.psum_scatter(out_term, "tp", scatter_dimension=2, tiled=True).astype(jnp.bfloat16)


VM = pl.BlockSpec(memory_space=pltpu.VMEM)
SM = pl.BlockSpec(memory_space=pltpu.SMEM)
HB = pl.BlockSpec(memory_space=pl.ANY)
DMA = pltpu.SemaphoreType.DMA
WIDE = 4 * HD
FAR = (7, 6, 5, 4)
NEAR = (3, 2, 1, 0)


def struct(shape, dtype):
    return jax.ShapeDtypeStruct(shape, dtype)


def call(kernel, out_shape, in_specs, *args, scratch=(), mib=16, nbytes=2e6, flops=1e6):
    single = not isinstance(out_shape, (list, tuple))
    return pl.pallas_call(
        kernel,
        out_shape=out_shape,
        in_specs=in_specs,
        out_specs=VM if single else [VM] * len(out_shape),
        scratch_shapes=list(scratch),
        compiler_params=pltpu.CompilerParams(vmem_limit_bytes=mib << 20),
        cost_estimate=pl.CostEstimate(
            flops=int(flops), bytes_accessed=int(nbytes), transcendentals=0
        ),
    )(*args)


def move(x, mask):
    count = lax.axis_size("tp")
    return lax.ppermute(x, "tp", [(i, i ^ mask) for i in range(count)])


def dot(a, b):
    return jnp.dot(a, b, preferred_element_type=F32)


def start_all(copies):
    for c in copies:
        c.start()


def wait_all(copies):
    for c in copies:
        c.wait()


def pick_columns(w, blocks, width):
    rows = w.shape[0]
    count = blocks.shape[0]

    def kernel(idx_ref, w_ref, o_ref, sem):
        copies = [
            pltpu.make_async_copy(
                w_ref.at[:, pl.ds(pl.multiple_of(idx_ref[i] * width, width), width)],
                o_ref.at[:, pl.ds(i * width, width)],
                sem.at[i],
            )
            for i in range(count)
        ]
        start_all(copies)
        wait_all(copies)

    return call(
        kernel,
        struct((rows, count * width), w.dtype),
        [SM, HB],
        blocks,
        w,
        scratch=[DMA((count,))],
        nbytes=4 * rows * count * width,
    )


def remote_terms(x, d, w, rows_a):
    a = dot(x[:rows_a, :], w[:, WIDE:])
    rest = jnp.concatenate([x[rows_a:, :], d[...]])
    b = [dot(rest, w[:, j * WIDE + HD : (j + 1) * WIDE]) for j in range(2)]
    return a, b


def kv_before(x0, d0, w0, rows_a):
    rows_b = x0.shape[0] - rows_a + d0.shape[0]

    def kernel(x, d, w, a_ref, b_ref):
        a, b = remote_terms(x, d, w, rows_a)
        a_ref[...] = a
        for j in range(2):
            b_ref[:, j * 3 * HD : (j + 1) * 3 * HD] = b[j]

    shapes = [struct((rows_a, WIDE), F32), struct((rows_b, 6 * HD), F32)]
    return call(kernel, shapes, [VM] * 3, x0, d0, w0, mib=20)


def kv_remote(pa, pb, x1, d0, d1, w1, rows_a):
    fresh, depth = d0.shape
    rows_b = pb.shape[0]
    folds = depth // (2 * HD)

    def kernel(pa, pb, x, d0, d1, w, a_ref, *b_refs):
        a, b = remote_terms(x, d1, w, rows_a)
        a_ref[...] = (pa[...] + a).astype(BF16)
        for j in range(2):
            t = (pb[:, j * 3 * HD : (j + 1) * 3 * HD] + b[j]).astype(BF16)
            for k in range(3):
                b_refs[k][:rows_b, j * HD : (j + 1) * HD] = t[:, k * HD : (k + 1) * HD]
        for k in range(3):
            for f in range(folds):
                b_refs[k][rows_b + f * fresh : rows_b + (f + 1) * fresh, :] = d0[
                    :, f * 2 * HD : (f + 1) * 2 * HD
                ]

    shapes = [struct((rows_a, WIDE), BF16)]
    shapes += [struct((rows_b + folds * fresh, 2 * HD), BF16)] * 3
    return call(kernel, shapes, [VM] * 6, pa, pb, x1, d0, d1, w1, mib=20)


def kv_local(x0, x1, d0, d1, w0, w1, rows_a):
    rows_b = x0.shape[0] - rows_a + d0.shape[0]

    def kernel(x0, x1, d0, d1, w0, w1, a_ref, b_ref):
        a_ref[...] = dot(x0[:rows_a, :], w0[:, :WIDE]) + dot(x1[:rows_a, :], w1[:, :WIDE])
        rest0 = jnp.concatenate([x0[rows_a:, :], d0[...]])
        rest1 = jnp.concatenate([x1[rows_a:, :], d1[...]])
        for j in range(2):
            cols = slice(j * WIDE, j * WIDE + HD)
            b_ref[:, j * HD : (j + 1) * HD] = dot(rest0, w0[:, cols]) + dot(rest1, w1[:, cols])

    shapes = [struct((rows_a, WIDE), F32), struct((rows_b, 2 * HD), F32)]
    return call(kernel, shapes, [VM] * 6, x0, x1, d0, d1, w0, w1, mib=20)


def mid_a(own, got):
    rows = own.shape[0]

    def kernel(own, got, m_ref, z1, z2, z3):
        for k, ref in ((0, m_ref), (1, z1), (2, z2), (3, z3)):
            cols = slice(k * HD, (k + 1) * HD)
            ref[...] = (own[:, cols] + got[:, cols].astype(F32)).astype(ref.dtype)

    shapes = [struct((rows, HD), F32)] + [struct((rows, HD), BF16)] * 3
    return call(kernel, shapes, [VM] * 2, own, got)


def mid_b(own, d0, g1, g2, g3):
    rows = own.shape[0]
    fresh, depth = d0.shape
    folds = depth // HD

    def kernel(own, d0, g1, g2, g3, m_ref, y_ref, s_ref):
        for j, ref in ((0, m_ref), (1, y_ref)):
            cols = slice(j * HD, (j + 1) * HD)
            total = own[:, cols]
            for g in (g1, g2, g3):
                total = total + g[:rows, cols].astype(F32)
            ref[:rows, :] = total.astype(ref.dtype)
        for k in range(4):
            for f in range(folds):
                if k == 0:
                    piece = d0[:, f * HD : (f + 1) * HD]
                else:
                    first = rows + f // 2 * fresh
                    piece = (g1, g2, g3)[k - 1][
                        first : first + fresh, f % 2 * HD : (f % 2 + 1) * HD
                    ]
                at = (k * folds + f) * fresh
                y_ref[rows + at : rows + at + fresh, :] = piece
                s_ref[at : at + fresh, :] = piece

    span = 4 * folds * fresh
    shapes = [struct((rows, HD), F32), struct((rows + span, HD), BF16), struct((span, HD), BF16)]
    return call(kernel, shapes, [VM] * 5, own, d0, g1, g2, g3)


def finish_kv(a_own, a1, a2, a3, b_own, b1, tokens):
    rows_a, rows_b = a_own.shape[0], b_own.shape[0]
    blocks = tokens // BLK
    rows = rows_a + rows_b

    def kernel(a_own, a1, a2, a3, b_own, b1, o_ref):
        a = a_own[...] + a1[...].astype(F32) + a2[...].astype(F32) + a3[...].astype(F32)
        b = b_own[...] + b1[:rows_b, :].astype(F32)
        for v, first in ((a, 0), (b[: tokens - rows_a], rows_a)):
            n = v.shape[0] // BLK
            v = v.reshape(n, BLK, HD)
            top = jnp.max(jnp.max(jnp.abs(v), axis=1, keepdims=True), axis=2, keepdims=True)
            scale = (top + 1e-06).astype(BF16)
            wide = jnp.broadcast_to(scale.astype(F32), (n, 1, HD))
            o_ref[first : first + n * BLK, :] = (v / wide).astype(BF16).reshape(n * BLK, HD)
            o_ref[rows + first // BLK : rows + first // BLK + n, :] = wide.reshape(n, HD).astype(
                BF16
            )
        o_ref[tokens:rows, :] = b[tokens - rows_a :].astype(BF16)

    shape = struct((rows + blocks, HD), BF16)
    return call(kernel, shape, [VM] * 6, a_own, a1, a2, a3, b_own, b1)


def queries_of(so, sx, first, side, rows, w_query, chip, core, acc=None):
    cols = w_query.shape[1]
    depth = w_query.shape[0] // 16
    folds = depth // HD
    starts = [(2 * (chip ^ (2 * k + side)) + (core ^ o)) * depth for k in range(4) for o in range(2)]
    starts = jnp.stack(starts).astype(jnp.int32)

    def kernel(idx, so, sx, w_ref, *rest):
        out, wbuf, sem = rest[-3:]
        copies = [
            pltpu.make_async_copy(
                w_ref.at[pl.ds(pl.multiple_of(idx[i], depth), depth), :], wbuf.at[i], sem.at[i]
            )
            for i in range(8)
        ]
        start_all(copies)
        total = rest[0][...] if acc is not None else jnp.zeros((rows, cols), F32)
        for k in range(4):
            for o, s in ((0, so), (1, sx)):
                lhs = jnp.concatenate(
                    [
                        s[first + (k * folds + f) * rows : first + (k * folds + f + 1) * rows, :]
                        for f in range(folds)
                    ],
                    axis=1,
                )
                copies[2 * k + o].wait()
                total = total + dot(lhs, wbuf[2 * k + o])
        out[...] = total.astype(out.dtype)

    extra = [] if acc is None else [acc]
    return call(
        kernel,
        struct((rows, cols), F32 if acc is None else BF16),
        [SM, VM, VM, HB] + [VM] * len(extra),
        starts,
        so,
        sx,
        w_query,
        *extra,
        scratch=[pltpu.VMEM((8, depth, cols), BF16), DMA((8,))],
        nbytes=5e6,
        flops=3e8,
    )


def weight_copies(idx, w_out, w_got, wbuf, sem, first):
    width = wbuf.shape[-1]
    copies = []
    for i in range(4):
        column = pl.ds(pl.multiple_of(idx[i] * width, width), width)
        copies.append(pltpu.make_async_copy(w_out.at[:, column], wbuf.at[i, 0], sem.at[i, 0]))
        column = pl.ds((first + i) * width, width)
        copies.append(pltpu.make_async_copy(w_got.at[:, column], wbuf.at[i, 1], sem.at[i, 1]))
    return copies


def weight_scratch(w_out, width):
    return [pltpu.VMEM((4, 2, w_out.shape[0], width), BF16), DMA((4, 2))]


def attend_far(q0, q1, kv0, kv1, marks, w_out, w_got, chip, core, tokens, row_count):
    rows, qcols = q0.shape
    heads = qcols // HD
    blocks = tokens // BLK
    slots = tokens + rows
    width = w_got.shape[1] // 8
    rate = math.log2(math.e) / math.sqrt(HD)
    order = jnp.stack([2 * (chip ^ r) + core for r in FAR] + [core]).astype(jnp.int32)

    def kernel(idx, q0, q1, kv0, kv1, mk, w_out, w_got, att0, att1, *rest):
        outs, wbuf, sem = rest[:4], rest[4], rest[5]
        copies = weight_copies(idx, w_out, w_got, wbuf, sem, 0)
        start_all(copies)
        first = idx[4] == 0

        def wide(kv):
            scale = kv[slots:, :].astype(F32).reshape(blocks, 1, HD)
            v = kv[:tokens, :].astype(F32).reshape(blocks, BLK, HD) * scale
            return v.reshape(tokens, HD).astype(BF16)

        own, oth = wide(kv0), wide(kv1)
        own_new, oth_new = kv0[tokens:slots, :], kv1[tokens:slots, :]
        keys = jnp.concatenate([jnp.where(first, own, oth), jnp.where(first, own_new, oth_new)])
        values = jnp.concatenate([jnp.where(first, oth, own), jnp.where(first, oth_new, own_new)])
        who = lax.broadcasted_iota(jnp.int32, (rows, slots), 0)
        seen = (lax.rem(who, row_count) == mk[0:1, :]) & (who >= mk[1:2, :])
        for q, att in ((q0, att0), (q1, att1)):
            stack = jnp.concatenate([q[:, g * HD : (g + 1) * HD] for g in range(heads)])
            score = lax.dot_general(
                stack, keys, (((1,), (1,)), ((), ())), preferred_element_type=F32
            )
            score = jnp.where(seen[None], score.reshape(heads, rows, slots), -jnp.inf)
            top = jnp.max(score, axis=2, keepdims=True)
            weight = jnp.exp2((score - top) * rate)
            total = jnp.sum(weight, axis=2, keepdims=True)
            mixed = dot(weight.astype(BF16).reshape(heads * rows, slots), values)
            mixed = mixed.reshape(heads, rows, HD) / total
            for g in range(heads):
                att[:, g * HD : (g + 1) * HD] = mixed[g].astype(BF16)
        for i in range(4):
            wait_all(copies[2 * i : 2 * i + 2])
            term = dot(att0[...], wbuf[i, 0]) + dot(att1[...], wbuf[i, 1])
            outs[i][...] = term.astype(BF16)

    shapes = [struct((rows, qcols), BF16)] * 2 + [struct((rows, width), BF16)] * 4
    return call(
        kernel,
        shapes,
        [SM] + [VM] * 5 + [HB] * 2,
        order,
        q0,
        q1,
        kv0,
        kv1,
        marks,
        w_out,
        w_got,
        scratch=weight_scratch(w_out, width),
        mib=32,
        flops=8e8,
        nbytes=5e6,
    )


def out_near(att0, att1, w_out, w_got, chip, core):
    rows = att0.shape[0]
    width = w_got.shape[1] // 8
    order = jnp.stack([2 * (chip ^ r) + core for r in NEAR]).astype(jnp.int32)

    def kernel(idx, att0, att1, w_out, w_got, *rest):
        outs, wbuf, sem = rest[:4], rest[4], rest[5]
        copies = weight_copies(idx, w_out, w_got, wbuf, sem, 4)
        start_all(copies)
        for i in range(4):
            wait_all(copies[2 * i : 2 * i + 2])
            term = dot(att0[...], wbuf[i, 0]) + dot(att1[...], wbuf[i, 1])
            outs[i][...] = term.astype(outs[i].dtype)

    shapes = [struct((rows, width), BF16)] * 3 + [struct((rows, width), F32)]
    return call(
        kernel,
        shapes,
        [SM, VM, VM, HB, HB],
        order,
        att0,
        att1,
        w_out,
        w_got,
        scratch=weight_scratch(w_out, width),
        flops=5e8,
        nbytes=5e6,
    )


def add_up(own, parts):
    def kernel(*refs):
        total = refs[0][...]
        for r in refs[1:-1]:
            total = total + r[...].astype(F32)
        refs[-1][...] = total.astype(BF16)

    return call(kernel, struct(own.shape, BF16), [VM] * (1 + len(parts)), own, *parts)


def paired(prompt_x, decode_x, w_query, w_keyval, w_out, prompt_blocks, prompt_row):
    return paired_body(
        prompt_x, decode_x, w_query, w_keyval, w_out, prompt_blocks, prompt_row
    )


def paired_body(prompt_x, decode_x, w_query, w_keyval, w_out, prompt_blocks, prompt_row):
    count = lax.axis_size("tp")
    index = lax.axis_index("tp")
    core, chip = index % 2, index // 2
    tokens = prompt_x.shape[0]
    steps, row_count, depth = decode_x.shape
    fresh = steps * row_count
    total_blocks = tokens // BLK
    rows_a = (tokens + fresh) * 3 // 4 // BLK * BLK
    rows_b = tokens - rows_a + fresh
    d_own = decode_x.reshape(fresh, depth)
    x_oth = move(prompt_x, 1)
    d_oth = move(d_own, 1)
    rel = [(i % 4) * 2 + i // 4 for i in range(8)]
    keep_cols = jnp.stack([(chip ^ r) * 2 + core for r in rel]).astype(jnp.int32)
    send_cols = jnp.stack([(chip ^ r) * 2 + 1 - core for r in rel]).astype(jnp.int32)
    w_oth = move(pick_columns(w_keyval, send_cols, HD), 1)
    w_keep = pick_columns(w_keyval, keep_cols, HD)
    pa, pb = kv_before(prompt_x, d_own, w_keep, rows_a)
    a_send, b1, b2, b3 = kv_remote(pa, pb, x_oth, d_own, d_oth, w_oth, rows_a)
    a_got = move(a_send, 2)
    g2, g3, g1 = move(b2, 8), move(b3, 12), move(b1, 4)
    a_own, b_own = kv_local(prompt_x, x_oth, d_own, d_oth, w_keep, w_oth, rows_a)
    width = w_out.shape[1] // count
    out_cols = jnp.stack([2 * (chip ^ r) + 1 - core for r in FAR + NEAR]).astype(jnp.int32)
    w_got = move(pick_columns(w_out, out_cols, width), 1)
    a_own, a1, a2, a3 = mid_a(a_own, a_got)
    h2 = move(a2, 8)
    b_own, y_send, s0 = mid_b(b_own, d_own, g1, g2, g3)
    y_got = move(y_send, 2)
    h3, h1 = move(a3, 12), move(a1, 4)
    s0_oth = move(s0, 1)
    acc = queries_of(s0, s0_oth, 0, 0, fresh, w_query, chip, core)
    y_oth = move(y_got, 1)
    q_own = queries_of(y_got, y_oth, rows_b, 1, fresh, w_query, chip, core, acc)
    q_oth = move(q_own, 1)
    slot_row = jnp.repeat(block_rows(prompt_blocks, prompt_row, total_blocks), BLK)
    new = jnp.arange(fresh, dtype=jnp.int32)
    marks = jnp.stack(
        [
            jnp.concatenate([slot_row, new % row_count]),
            jnp.concatenate([jnp.zeros_like(slot_row), new // row_count * row_count]),
        ]
    )
    kv_own = finish_kv(a_own, h1, h2, h3, b_own, y_got, tokens)
    kv_oth = move(kv_own, 1)
    att0, att1, *far = attend_far(
        q_own, q_oth, kv_own, kv_oth, marks, w_out, w_got, chip, core, tokens, row_count
    )
    *near, mine = out_near(att0, att1, w_out, w_got, chip, core)
    parts = [move(s, 2 * r) for r, s in zip(FAR + NEAR, far + near)]
    return add_up(mine, parts).reshape(steps, row_count, width)


def solution(mesh):
    placed = (
        P(("group", "pool"), "tp"),
        P(None, ("group", "pool"), "tp"),
        P(None, "tp"),
        P("tp", None),
        P("tp", None),
        P("group"),
        P("group"),
    )
    pairs = mesh.shape["pool"] == 1 and mesh.shape["tp"] == 2 * KVH
    return jax.shard_map(
        paired if pairs else general,
        mesh=mesh,
        in_specs=placed,
        out_specs=P(None, ("group", "pool"), "tp"),
        check_vma=False,
    )
```

```python
import math

import jax
import jax.numpy as jnp
import numpy as np
from jax import lax
from jax.experimental import pallas as pl
from jax.experimental.pallas import tpu as pltpu
from jax.sharding import PartitionSpec as P


KVH = 8
HD = 128
BLK = 16
F32 = jnp.float32
BF16 = jnp.bfloat16


def block_rows(prompt_blocks, prompt_row, total_blocks):
    block_ends = jnp.cumsum(prompt_blocks)
    positions = jnp.arange(total_blocks, dtype=jnp.int32)
    owner_seq = jnp.sum((block_ends[None, :] <= positions[:, None]).astype(jnp.int32), axis=1)
    seq_match = owner_seq[:, None] == jnp.arange(prompt_row.shape[0], dtype=jnp.int32)[None, :]
    return jnp.sum(jnp.where(seq_match, prompt_row[None, :], 0), axis=1)


def attend(queries, cache_vals, cache_scale, slot_row, fresh_keyval, row_ids):
    head_dim = queries.shape[-1]
    inverse_root = 1.0 / math.sqrt(head_dim)
    query_f32 = queries.astype(jnp.float32)
    scale_f32 = cache_scale.astype(jnp.float32)
    cache_keys = cache_vals[:, :, :head_dim].astype(jnp.float32) * scale_f32[:, 0][:, None, None]
    cache_values = cache_vals[:, :, head_dim:].astype(jnp.float32) * scale_f32[:, 1][:, None, None]
    cache_score = jnp.einsum("srgd,nkd->srgnk", query_f32, cache_keys) * inverse_root
    visible = slot_row[None, :] == row_ids[:, None]
    cache_score = jnp.where(visible[None, :, None, :, None], cache_score, -jnp.inf)
    fresh_f32 = fresh_keyval.astype(jnp.float32)
    fresh_score = jnp.einsum("srgd,trd->srgt", query_f32, fresh_f32[:, :, :head_dim]) * inverse_root
    step_index = jnp.arange(queries.shape[0], dtype=jnp.int32)
    causal = step_index[:, None] >= step_index[None, :]
    fresh_score = jnp.where(causal[:, None, None, :], fresh_score, -jnp.inf)
    top_score = jnp.maximum(jnp.max(cache_score, axis=(3, 4)), jnp.max(fresh_score, axis=3))
    cache_weight = jnp.exp(cache_score - top_score[..., None, None])
    fresh_weight = jnp.exp(fresh_score - top_score[..., None])
    denominator = jnp.sum(cache_weight, axis=(3, 4)) + jnp.sum(fresh_weight, axis=3)
    weighted = jnp.einsum("srgnk,nkd->srgd", cache_weight, cache_values)
    weighted = weighted + jnp.einsum("srgt,trd->srgd", fresh_weight, fresh_f32[:, :, head_dim:])
    return weighted / denominator[..., None]


def general(prompt_x, decode_x, w_query, w_keyval, w_out, prompt_blocks, prompt_row):
    tp_count = lax.axis_size("tp")
    pool_count = lax.axis_size("pool")
    tp_index = lax.axis_index("tp")
    pool_index = lax.axis_index("pool")
    half_tokens = prompt_x.shape[0]
    tokens_here = half_tokens // tp_count
    blocks_here = tokens_here // BLK
    half_blocks = half_tokens // BLK
    total_blocks = half_blocks * pool_count
    keyval = lax.psum_scatter(
        jnp.dot(prompt_x, w_keyval, preferred_element_type=jnp.float32),
        "tp",
        scatter_dimension=0,
        tiled=True,
    )
    blocked = keyval.reshape(blocks_here, BLK, KVH, 2, HD)
    scales = (jnp.max(jnp.abs(blocked), axis=(1, 4)) + 1e-06).astype(jnp.bfloat16)
    stored = (blocked / scales.astype(jnp.float32)[:, None, :, :, None]).astype(jnp.bfloat16)
    stored = stored.reshape(blocks_here, BLK, KVH, 2 * HD)
    slot_row_all = block_rows(prompt_blocks, prompt_row, total_blocks)
    row_half = decode_x.shape[1]
    owner_half = slot_row_all // row_half
    first_block = pool_index * half_blocks + tp_index * blocks_here
    mine_owner = lax.dynamic_slice_in_dim(owner_half, first_block, blocks_here, 0)
    dest_head = np.arange(tp_count) * KVH // tp_count
    by_head = stored.transpose(2, 0, 1, 3)[dest_head]
    scale_head = scales.transpose(1, 0, 2)[dest_head]
    to_half = mine_owner[None, :] == jnp.arange(pool_count, dtype=jnp.int32)[:, None]
    zero_value = jnp.zeros((), jnp.bfloat16)
    send_vals = jnp.where(to_half[None, :, :, None, None], by_head[:, None], zero_value)
    send_scale = jnp.where(to_half[None, :, :, None], scale_head[:, None], zero_value)
    got_vals, got_scale = (
        lax.all_to_all(
            lax.all_to_all(sent, "tp", split_axis=0, concat_axis=0, tiled=True),
            "pool",
            split_axis=1,
            concat_axis=1,
            tiled=True,
        )
        for sent in (send_vals, send_scale)
    )
    got_vals = got_vals.reshape(total_blocks, BLK, 2 * HD)
    got_scale = got_scale.reshape(total_blocks, 2)
    slot_row = (
        slot_row_all.reshape(pool_count, tp_count, blocks_here)
        .transpose(1, 0, 2)
        .reshape(total_blocks)
    )
    gathered = lax.all_gather(decode_x, "tp", axis=2, tiled=True)
    step_count, row_count, _ = gathered.shape
    heads_here = w_query.shape[1] // HD
    queries = jnp.einsum("srd,de->sre", gathered, w_query, preferred_element_type=jnp.float32)
    queries = queries.astype(jnp.bfloat16).reshape(step_count, row_count, heads_here, HD)
    partial_new = jnp.einsum("srd,de->sre", decode_x, w_keyval, preferred_element_type=jnp.float32)
    summed_new = lax.psum(partial_new, "tp")
    fresh_keyval = summed_new.astype(jnp.bfloat16).reshape(step_count, row_count, KVH, 2 * HD)
    my_head = tp_index * KVH // tp_count
    fresh_keyval = lax.dynamic_index_in_dim(fresh_keyval, my_head, 2, keepdims=False)
    row_ids = pool_index * row_count + jnp.arange(row_count, dtype=jnp.int32)
    weighted = attend(queries, got_vals, got_scale, slot_row, fresh_keyval, row_ids)
    attended = weighted.reshape(step_count, row_count, heads_here * HD).astype(jnp.bfloat16)
    out_term = jnp.einsum("sre,ed->srd", attended, w_out, preferred_element_type=jnp.float32)
    return lax.psum_scatter(out_term, "tp", scatter_dimension=2, tiled=True).astype(jnp.bfloat16)


VM = pl.BlockSpec(memory_space=pltpu.VMEM)
SM = pl.BlockSpec(memory_space=pltpu.SMEM)
HB = pl.BlockSpec(memory_space=pltpu.HBM)
DMA = pltpu.SemaphoreType.DMA
WIDE = 4 * HD
FULL = 50
FAR = (7, 6, 5, 4)
NEAR = (3, 2, 1, 0)
REL = (0, 2, 4, 6, 1, 3, 5, 7)


def struct(shape, dtype):
    return jax.ShapeDtypeStruct(shape, dtype)


def call(kernel, out_shape, in_specs, *args, scratch=(), mib=16, nbytes=2e6, flops=1e6):
    single = not isinstance(out_shape, (list, tuple))
    return pl.pallas_call(
        kernel,
        out_shape=out_shape,
        in_specs=in_specs,
        out_specs=VM if single else [VM] * len(out_shape),
        scratch_shapes=list(scratch),
        compiler_params=pltpu.CompilerParams(vmem_limit_bytes=mib << 20),
        cost_estimate=pl.CostEstimate(
            flops=int(flops), bytes_accessed=int(nbytes), transcendentals=0
        ),
    )(*args)


def move(x, mask):
    count = lax.axis_size("tp")
    return lax.ppermute(x, "tp", [(i, i ^ mask) for i in range(count)])


def dot(a, b):
    return jnp.dot(a, b, preferred_element_type=F32)


def start_all(copies):
    for c in copies:
        c.start()


def wait_all(copies):
    for c in copies:
        c.wait()


def column_copies(w, out, sem, columns, width):
    return [
        pltpu.make_async_copy(
            w.at[:, pl.ds(pl.multiple_of(c * width, width), width)],
            out.at[:, pl.ds(i * width, width)],
            sem.at[i],
        )
        for i, c in enumerate(columns)
    ]


def pick_columns(ids, w, rel, width):
    rows = w.shape[0]

    def kernel(ids, w, o_ref, sem):
        copies = column_copies(w, o_ref, sem, [2 * (ids[0] ^ r) + 1 - ids[1] for r in rel], width)
        start_all(copies)
        wait_all(copies)

    size = rows * len(rel) * width
    return call(
        kernel,
        struct((rows, len(rel) * width), w.dtype),
        [SM, HB],
        ids,
        w,
        scratch=[DMA((len(rel),))],
        nbytes=4 * size,
    )


def remote_terms(x, d, w, rows_a):
    a = dot(x[:rows_a, :], w[:, WIDE:])
    rest = jnp.concatenate([x[rows_a:, :], d[...]])
    b = [dot(rest, w[:, j * WIDE + HD : (j + 1) * WIDE]) for j in range(2)]
    return a, b


def kv_load(ids, w, x0, d0):
    rows = w.shape[0]

    def kernel(ids, w, x0, d0, o_ref, k_ref, x_ref, d_ref, osem, ksem, xsem):
        copies = []
        for ref, sem, core in ((o_ref, osem, 1 - ids[1]), (k_ref, ksem, ids[1])):
            copies += column_copies(w, ref, sem, [2 * (ids[0] ^ r) + core for r in REL], HD)
        copies.append(pltpu.make_async_copy(x0, x_ref, xsem.at[0]))
        copies.append(pltpu.make_async_copy(d0, d_ref, xsem.at[1]))
        start_all(copies)
        wait_all(copies)

    shapes = [struct((rows, 8 * HD), BF16)] * 2 + [struct(a.shape, BF16) for a in (x0, d0)]
    scratch = [DMA((8,)), DMA((8,)), DMA((2,))]
    specs = [SM, HB, HB, HB]
    return call(kernel, shapes, specs, ids, w, x0, d0, scratch=scratch, mib=FULL)


def kv_before(x0, d0, w0, rows_a):
    rows_b = x0.shape[0] - rows_a + d0.shape[0]

    def kernel(x, d, w, a_ref, b_ref):
        a, b = remote_terms(x, d, w, rows_a)
        a_ref[...] = a
        for j in range(2):
            b_ref[:, j * 3 * HD : (j + 1) * 3 * HD] = b[j]

    shapes = [struct((rows_a, WIDE), F32), struct((rows_b, 6 * HD), F32)]
    return call(kernel, shapes, [VM] * 3, x0, d0, w0, mib=20)


def kv_remote(pa, pb, x1, d0, d1, w1, rows_a):
    fresh, depth = d0.shape
    rows_b = pb.shape[0]
    folds = depth // (2 * HD)

    def kernel(pa, pb, x, d0, d1, w, a_ref, *b_refs):
        a, b = remote_terms(x, d1, w, rows_a)
        a_ref[...] = (pa[...] + a).astype(BF16)
        for j in range(2):
            t = (pb[:, j * 3 * HD : (j + 1) * 3 * HD] + b[j]).astype(BF16)
            for k in range(3):
                b_refs[k][:rows_b, j * HD : (j + 1) * HD] = t[:, k * HD : (k + 1) * HD]
        for k in range(3):
            for f in range(folds):
                b_refs[k][rows_b + f * fresh : rows_b + (f + 1) * fresh, :] = d0[
                    :, f * 2 * HD : (f + 1) * 2 * HD
                ]

    shapes = [struct((rows_a, WIDE), BF16)]
    shapes += [struct((rows_b + folds * fresh, 2 * HD), BF16)] * 3
    return call(kernel, shapes, [VM] * 6, pa, pb, x1, d0, d1, w1, mib=20)


def kv_local(x0, x1, d0, d1, w0, w1, rows_a):
    rows_b = x0.shape[0] - rows_a + d0.shape[0]

    def kernel(x0, x1, d0, d1, w0, w1, a_ref, b_ref):
        a_ref[...] = dot(x0[:rows_a, :], w0[:, :WIDE]) + dot(x1[:rows_a, :], w1[:, :WIDE])
        rest0 = jnp.concatenate([x0[rows_a:, :], d0[...]])
        rest1 = jnp.concatenate([x1[rows_a:, :], d1[...]])
        for j in range(2):
            cols = slice(j * WIDE, j * WIDE + HD)
            b_ref[:, j * HD : (j + 1) * HD] = dot(rest0, w0[:, cols]) + dot(rest1, w1[:, cols])

    shapes = [struct((rows_a, WIDE), F32), struct((rows_b, 2 * HD), F32)]
    return call(kernel, shapes, [VM] * 6, x0, x1, d0, d1, w0, w1, mib=20)


def mid_a(own, got):
    rows = own.shape[0]

    def kernel(own, got, m_ref, z1, z2, z3):
        for k, ref in ((0, m_ref), (1, z1), (2, z2), (3, z3)):
            cols = slice(k * HD, (k + 1) * HD)
            ref[...] = (own[:, cols] + got[:, cols].astype(F32)).astype(ref.dtype)

    shapes = [struct((rows, HD), F32)] + [struct((rows, HD), BF16)] * 3
    return call(kernel, shapes, [VM] * 2, own, got)


def mid_b(own, d0, g1, g2, g3):
    rows = own.shape[0]
    fresh, depth = d0.shape
    folds = depth // HD

    def kernel(own, d0, g1, g2, g3, m_ref, y_ref, s_ref):
        for j, ref in ((0, m_ref), (1, y_ref)):
            cols = slice(j * HD, (j + 1) * HD)
            total = own[:, cols]
            for g in (g1, g2, g3):
                total = total + g[:rows, cols].astype(F32)
            ref[:rows, :] = total.astype(ref.dtype)
        for k in range(4):
            for f in range(folds):
                if k == 0:
                    piece = d0[:, f * HD : (f + 1) * HD]
                else:
                    first = rows + f // 2 * fresh
                    piece = (g1, g2, g3)[k - 1][
                        first : first + fresh, f % 2 * HD : (f % 2 + 1) * HD
                    ]
                at = (k * folds + f) * fresh
                y_ref[rows + at : rows + at + fresh, :] = piece
                s_ref[at : at + fresh, :] = piece

    span = 4 * folds * fresh
    shapes = [struct((rows, HD), F32), struct((rows + span, HD), BF16), struct((span, HD), BF16)]
    return call(kernel, shapes, [VM] * 5, own, d0, g1, g2, g3)


def finish_kv(a_own, a1, a2, a3, b_own, b1, tokens):
    rows_a, rows_b = a_own.shape[0], b_own.shape[0]
    blocks = tokens // BLK
    rows = rows_a + rows_b

    def kernel(a_own, a1, a2, a3, b_own, b1, o_ref):
        a = a_own[...] + a1[...].astype(F32) + a2[...].astype(F32) + a3[...].astype(F32)
        b = b_own[...] + b1[:rows_b, :].astype(F32)
        for v, first in ((a, 0), (b[: tokens - rows_a], rows_a)):
            n = v.shape[0] // BLK
            v = v.reshape(n, BLK, HD)
            top = jnp.max(jnp.max(jnp.abs(v), axis=1, keepdims=True), axis=2, keepdims=True)
            scale = (top + 1e-06).astype(BF16)
            wide = jnp.broadcast_to(scale.astype(F32), (n, 1, HD))
            o_ref[first : first + n * BLK, :] = (v / wide).astype(BF16).reshape(n * BLK, HD)
            o_ref[rows + first // BLK : rows + first // BLK + n, :] = wide.reshape(n, HD).astype(
                BF16
            )
        o_ref[tokens:rows, :] = b[tokens - rows_a :].astype(BF16)

    shape = struct((rows + blocks, HD), BF16)
    return call(kernel, shape, [VM] * 6, a_own, a1, a2, a3, b_own, b1)


def queries_of(ids, so, sx, first, side, rows, w_query, acc=None):
    cols = w_query.shape[1]
    depth = w_query.shape[0] // 16
    folds = depth // HD

    def kernel(ids, so, sx, w_ref, *rest):
        out, wbuf, sem = rest[-3:]
        copies = []
        for k in range(4):
            for o in range(2):
                at = (2 * (ids[0] ^ (2 * k + side)) + (ids[1] ^ o)) * depth
                copies.append(
                    pltpu.make_async_copy(
                        w_ref.at[pl.ds(pl.multiple_of(at, depth), depth), :],
                        wbuf.at[2 * k + o],
                        sem.at[2 * k + o],
                    )
                )
        start_all(copies)
        total = rest[0][...] if acc is not None else jnp.zeros((rows, cols), F32)
        for k in range(4):
            for o, s in ((0, so), (1, sx)):
                lhs = jnp.concatenate(
                    [
                        s[first + (k * folds + f) * rows : first + (k * folds + f + 1) * rows, :]
                        for f in range(folds)
                    ],
                    axis=1,
                )
                copies[2 * k + o].wait()
                total = total + dot(lhs, wbuf[2 * k + o])
        out[...] = total.astype(out.dtype)

    extra = [] if acc is None else [acc]
    return call(
        kernel,
        struct((rows, cols), F32 if acc is None else BF16),
        [SM, VM, VM, HB] + [VM] * len(extra),
        ids,
        so,
        sx,
        w_query,
        *extra,
        scratch=[pltpu.VMEM((8, depth, cols), BF16), DMA((8,))],
        nbytes=5e6,
        flops=3e8,
    )


def weight_copies(ids, w_out, w_got, wbuf, sem, rel, first):
    width = wbuf.shape[-1]
    copies = []
    for i, r in enumerate(rel):
        at = (2 * (ids[0] ^ r) + ids[1]) * width
        column = pl.ds(pl.multiple_of(at, width), width)
        copies.append(pltpu.make_async_copy(w_out.at[:, column], wbuf.at[i, 0], sem.at[i, 0]))
        column = pl.ds((first + i) * width, width)
        copies.append(pltpu.make_async_copy(w_got.at[:, column], wbuf.at[i, 1], sem.at[i, 1]))
    return copies


def weight_scratch(w_out, width):
    return [pltpu.VMEM((4, 2, w_out.shape[0], width), BF16), DMA((4, 2))]


def attend_far(ids, blocks_of, row_of, q0, q1, kv0, kv1, w_out, w_got, tokens, row_count):
    rows, qcols = q0.shape
    heads = qcols // HD
    blocks = tokens // BLK
    slots = tokens + rows
    width = w_got.shape[1] // 8
    rate = math.log2(math.e) / math.sqrt(HD)
    prompts = blocks_of.shape[0]

    def kernel(ids, num, own_row, q0, q1, kv0, kv1, w_out, w_got, att0, att1, *rest):
        outs, wbuf, sem = rest[:4], rest[4], rest[5]
        copies = weight_copies(ids, w_out, w_got, wbuf, sem, FAR, 0)
        start_all(copies)
        first = ids[1] == 0

        def wide(kv):
            scale = kv[slots:, :].astype(F32).reshape(blocks, 1, HD)
            v = kv[:tokens, :].astype(F32).reshape(blocks, BLK, HD) * scale
            return v.reshape(tokens, HD).astype(BF16)

        own, oth = wide(kv0), wide(kv1)
        own_new, oth_new = kv0[tokens:slots, :], kv1[tokens:slots, :]
        keys = jnp.concatenate([jnp.where(first, own, oth), jnp.where(first, own_new, oth_new)])
        values = jnp.concatenate([jnp.where(first, oth, own), jnp.where(first, oth_new, own_new)])
        slot = lax.broadcasted_iota(jnp.int32, (1, slots), 1)
        fresh = slot - tokens
        slot_row = lax.rem(fresh, row_count)
        since = jnp.where(fresh >= 0, fresh - slot_row, 0)
        end = 0
        for p in range(prompts):
            begin, end = end, end + num[p] * BLK
            slot_row = jnp.where((slot >= begin) & (slot < end), own_row[p], slot_row)
        who = lax.broadcasted_iota(jnp.int32, (rows, slots), 0)
        seen = (lax.rem(who, row_count) == slot_row) & (who >= since)
        for q, att in ((q0, att0), (q1, att1)):
            stack = jnp.concatenate([q[:, g * HD : (g + 1) * HD] for g in range(heads)])
            score = lax.dot_general(
                stack, keys, (((1,), (1,)), ((), ())), preferred_element_type=F32
            )
            score = jnp.where(seen[None], score.reshape(heads, rows, slots), -jnp.inf)
            top = jnp.max(score, axis=2, keepdims=True)
            weight = jnp.exp2((score - top) * rate)
            total = jnp.sum(weight, axis=2, keepdims=True)
            mixed = dot(weight.astype(BF16).reshape(heads * rows, slots), values)
            mixed = mixed.reshape(heads, rows, HD) / total
            for g in range(heads):
                att[:, g * HD : (g + 1) * HD] = mixed[g].astype(BF16)
        for i in range(4):
            wait_all(copies[2 * i : 2 * i + 2])
            term = dot(att0[...], wbuf[i, 0]) + dot(att1[...], wbuf[i, 1])
            outs[i][...] = term.astype(BF16)

    shapes = [struct((rows, qcols), BF16)] * 2 + [struct((rows, width), BF16)] * 4
    return call(
        kernel,
        shapes,
        [SM] * 3 + [VM] * 4 + [HB] * 2,
        ids,
        blocks_of,
        row_of,
        q0,
        q1,
        kv0,
        kv1,
        w_out,
        w_got,
        scratch=weight_scratch(w_out, width),
        mib=32,
        flops=8e8,
        nbytes=5e6,
    )


def out_near(ids, att0, att1, w_out, w_got):
    rows = att0.shape[0]
    width = w_got.shape[1] // 8

    def kernel(ids, att0, att1, w_out, w_got, *rest):
        outs, wbuf, sem = rest[:4], rest[4], rest[5]
        copies = weight_copies(ids, w_out, w_got, wbuf, sem, NEAR, 4)
        start_all(copies)
        for i in range(4):
            wait_all(copies[2 * i : 2 * i + 2])
            term = dot(att0[...], wbuf[i, 0]) + dot(att1[...], wbuf[i, 1])
            outs[i][...] = term.astype(outs[i].dtype)

    shapes = [struct((rows, width), BF16)] * 3 + [struct((rows, width), F32)]
    return call(
        kernel,
        shapes,
        [SM, VM, VM, HB, HB],
        ids,
        att0,
        att1,
        w_out,
        w_got,
        scratch=weight_scratch(w_out, width),
        flops=5e8,
        nbytes=5e6,
    )


def add_up(own, parts):
    def kernel(*refs):
        total = refs[0][...]
        for r in refs[1:-1]:
            total = total + r[...].astype(F32)
        refs[-1][...] = total.astype(BF16)

    return call(kernel, struct(own.shape, BF16), [VM] * (1 + len(parts)), own, *parts)


def paired(prompt_x, decode_x, w_query, w_keyval, w_out, prompt_blocks, prompt_row):
    return paired_body(
        prompt_x, decode_x, w_query, w_keyval, w_out, prompt_blocks, prompt_row
    )


def paired_body(prompt_x, decode_x, w_query, w_keyval, w_out, prompt_blocks, prompt_row):
    count = lax.axis_size("tp")
    index = lax.axis_index("tp")
    ids = jnp.stack([index // 2, index % 2]).astype(jnp.int32)
    tokens = prompt_x.shape[0]
    steps, row_count, depth = decode_x.shape
    fresh = steps * row_count
    rows_a = (tokens + fresh) * 3 // 4 // BLK * BLK
    rows_b = tokens - rows_a + fresh
    d_hbm = decode_x.reshape(fresh, depth)
    x_oth = move(prompt_x, 1)
    d_oth = move(d_hbm, 1)
    w_send, w_keep, x_own, d_own = kv_load(ids, w_keyval, prompt_x, d_hbm)
    w_oth = move(w_send, 1)
    pa, pb = kv_before(x_own, d_own, w_keep, rows_a)
    a_send, b1, b2, b3 = kv_remote(pa, pb, x_oth, d_own, d_oth, w_oth, rows_a)
    a_got = move(a_send, 2)
    g2, g3, g1 = move(b2, 8), move(b3, 12), move(b1, 4)
    a_own, b_own = kv_local(x_own, x_oth, d_own, d_oth, w_keep, w_oth, rows_a)
    width = w_out.shape[1] // count
    w_got = move(pick_columns(ids, w_out, FAR + NEAR, width), 1)
    a_own, a1, a2, a3 = mid_a(a_own, a_got)
    h2 = move(a2, 8)
    b_own, y_send, s0 = mid_b(b_own, d_own, g1, g2, g3)
    y_got = move(y_send, 2)
    h3, h1 = move(a3, 12), move(a1, 4)
    s0_oth = move(s0, 1)
    acc = queries_of(ids, s0, s0_oth, 0, 0, fresh, w_query)
    y_oth = move(y_got, 1)
    q_own = queries_of(ids, y_got, y_oth, rows_b, 1, fresh, w_query, acc)
    q_oth = move(q_own, 1)
    kv_own = finish_kv(a_own, h1, h2, h3, b_own, y_got, tokens)
    kv_oth = move(kv_own, 1)
    att0, att1, *far = attend_far(
        ids, prompt_blocks, prompt_row, q_own, q_oth, kv_own, kv_oth, w_out, w_got, tokens, row_count
    )
    *near, mine = out_near(ids, att0, att1, w_out, w_got)
    parts = [move(s, 2 * r) for r, s in zip(FAR + NEAR, far + near)]
    return add_up(mine, parts).reshape(steps, row_count, width)


def solution(mesh):
    placed = (
        P(("group", "pool"), "tp"),
        P(None, ("group", "pool"), "tp"),
        P(None, "tp"),
        P("tp", None),
        P("tp", None),
        P("group"),
        P("group"),
    )
    pairs = mesh.shape["pool"] == 1 and mesh.shape["tp"] == 2 * KVH
    return jax.shard_map(
        paired if pairs else general,
        mesh=mesh,
        in_specs=placed,
        out_specs=P(None, ("group", "pool"), "tp"),
        check_vma=False,
    )
```
